32 devices in a mesh: fifth: 4 (over y, x), space: 8 (over z, core).
Axes of the slice: x: 2, y: 2, z: 4, core: 2. Of those that a mesh axis runs over, the one named last changes fastest.
Arguments:
- spinor: float32 [8, 24, 8, 512], P('fifth', None, 'space'), may hold values from -6 to 6
- gauge_links: float32 [4, 18, 8, 512], P(None, None, 'space'), may hold values from -1 to 1, as said below
Outputs:
- filtered: float32 [8, 24, 8, 512], P('fifth', None, 'space')
The draws below stay inside these ranges and needn't reach their ends.
Inputs may be any that keep to these rules, and one draw needn't show every extreme that they name: `gauge_links`: every link is a special unitary 3 x 3 complex matrix.
All inputs are finite; a program needn't handle non-finite values.
Results may differ from the reference program's by a relative error of at most 0.00002.
Values sent between devices are 32-bit elements; how exact they have to be, the bound alone decides.
No kernel may reach another device: no remote copies, remote signals or barrier semaphores. Data moves between devices by JAX's collectives and lax.ppermute only.
A program may use at most 64 MiB of HBM per device.

```python
import jax
import jax.numpy as jnp
import numpy as np

L = 8
DEGREE = 4
SITES = 512
NT = 8
L5 = 8


def normalise(vectors):
    length = jnp.sqrt(jnp.sum(vectors * vectors, axis=(1, 2), keepdims=True))
    return vectors / length


def draw_gauge_links(key, part):
    first_key = jax.random.fold_in(key, 11)
    second_key = jax.random.fold_in(key, 23)
    shape = (4, 3, 2, NT, SITES)
    first = jnp.clip(0.6 * jax.random.normal(first_key, shape, jnp.float32), -1.0, 1.0)
    second = jnp.clip(0.6 * jax.random.normal(second_key, shape, jnp.float32), -1.0, 1.0)
    first_offset = np.zeros((1, 3, 2, 1, 1), np.float32)
    first_offset[0, 0, 0, 0, 0] = 3.0
    second_offset = np.zeros((1, 3, 2, 1, 1), np.float32)
    second_offset[0, 1, 0, 0, 0] = 3.0
    first = first + jnp.asarray(first_offset)
    second = second + jnp.asarray(second_offset)
    unit_one = normalise(first)
    one_re = unit_one[:, :, 0]
    one_im = unit_one[:, :, 1]
    second_re = second[:, :, 0]
    second_im = second[:, :, 1]
    inner_re = jnp.sum(one_re * second_re + one_im * second_im, axis=1, keepdims=True)
    inner_im = jnp.sum(one_re * second_im - one_im * second_re, axis=1, keepdims=True)
    rest_re = second_re - (inner_re * one_re - inner_im * one_im)
    rest_im = second_im - (inner_re * one_im + inner_im * one_re)
    unit_two = normalise(jnp.stack([rest_re, rest_im], axis=2))
    two_re = unit_two[:, :, 0]
    two_im = unit_two[:, :, 1]
    third_rows = []
    for index in range(3):
        left = (index + 1) % 3
        right = (index + 2) % 3
        cross_re = one_re[:, left] * two_re[:, right] - one_im[:, left] * two_im[:, right] - (one_re[:, right] * two_re[:, left] - one_im[:, right] * two_im[:, left])
        cross_im = one_re[:, left] * two_im[:, right] + one_im[:, left] * two_re[:, right] - (one_re[:, right] * two_im[:, left] + one_im[:, right] * two_re[:, left])
        third_rows.append(jnp.stack([cross_re, -cross_im], axis=1))
    unit_three = jnp.stack(third_rows, axis=1)
    matrix = jnp.stack([unit_one, unit_two, unit_three], axis=1)
    return matrix.reshape(4, 18, NT, SITES).astype(jnp.float32)


def shard_levels(stream_key, shape, cuts, least, top_value):
    def one(dim, blocks):
        steps = jax.random.uniform(jax.random.fold_in(jax.random.fold_in(stream_key, 6), dim), (blocks,), jnp.float32, least / len(cuts), top_value / len(cuts))
        return jnp.repeat(jnp.exp(steps), shape[dim] // blocks).reshape((-1,) + (1,) * (len(shape) - dim - 1))

    loudness = one(*cuts[0])
    for cut in cuts[1:]:
        loudness = loudness * one(*cut)
    return loudness


def bell_draw(rng, shape, scale, bound, shards=(), kind=jnp.bfloat16):
    loudness = shard_levels(rng, shape, shards, -0.22, 0.18) if shards else 1.0
    drawn = jax.random.normal(rng, shape, jnp.float32) * scale * loudness
    return jnp.minimum(jnp.maximum(drawn, -bound), bound).astype(kind)


def setup_inputs(seed: int = 0) -> dict:
    key_list = jax.random.split(jax.random.key(seed), 3)
    spinor = bell_draw(key_list[0], (L5, 24, NT, SITES), 1.0, 6.0, ((0, 4), (2, 8)), jnp.float32)
    gauge_links = draw_gauge_links(jax.random.fold_in(key_list[2], 71), 0)
    return {"spinor": spinor, "gauge_links": gauge_links}


wall_height = 1.8
quark_mass = 0.1
filter_center = 0.5
filter_radius = 8.0

gamma_block = (((1, 1), (0, 1)), ((1, 2), (0, 0)), ((0, 1), (1, 3)), ((0, 0), (1, 0)))
gamma_adjoint = (((1, 3), (0, 3)), ((1, 0), (0, 2)), ((0, 3), (1, 1)), ((0, 0), (1, 0)))


def times_unit(values, quarter):
    for repeat in range(quarter % 4):
        values = jnp.stack([-values[..., 1, :, :], values[..., 0, :, :]], axis=-3)
    return values


def project(current, direction, parity):
    halves_list = []
    for top_row in range(2):
        source, quarter = gamma_block[direction][top_row]
        blended = times_unit(current[..., 2 + source, :, :, :, :], quarter)
        halves_list.append(current[..., top_row, :, :, :, :] + parity * blended)
    return jnp.stack(halves_list, axis=-5)


def rebuild(half_spinor, direction, parity):
    lower_part = []
    for row_index in range(2):
        source, quarter = gamma_adjoint[direction][row_index]
        lower_part.append(parity * times_unit(half_spinor[..., source, :, :, :, :], quarter))
    return jnp.concatenate([half_spinor, jnp.stack(lower_part, axis=-5)], axis=-5)


def colour_mul(link_matrix, half_spinor, dagger):
    link_re = link_matrix[:, :, 0]
    link_im = link_matrix[:, :, 1]
    if dagger:
        link_re = jnp.swapaxes(link_re, 0, 1)
        link_im = -jnp.swapaxes(link_im, 0, 1)
    result_re = None
    result_im = None
    for column in range(3):
        half_re = half_spinor[..., column:column + 1, 0, :, :]
        half_im = half_spinor[..., column:column + 1, 1, :, :]
        term_re = link_re[:, column] * half_re - link_im[:, column] * half_im
        term_im = link_re[:, column] * half_im + link_im[:, column] * half_re
        if result_re is None:
            result_re, result_im = term_re, term_im
        else:
            result_re = result_re + term_re
            result_im = result_im + term_im
    return jnp.stack([result_re, result_im], axis=-3)


def space_shift(values, stride, extent, forward):
    position = (jnp.arange(values.shape[-1]) // stride) % extent
    if forward:
        inside_roll = jnp.roll(values, -stride, axis=-1)
        outside_roll = jnp.roll(values, (extent - 1) * stride, axis=-1)
        return jnp.where(position == extent - 1, outside_roll, inside_roll)
    inside_roll = jnp.roll(values, stride, axis=-1)
    outside_roll = jnp.roll(values, -(extent - 1) * stride, axis=-1)
    return jnp.where(position == 0, outside_roll, inside_roll)


def space_hops(current, gauge, extent):
    summed = jnp.zeros_like(current)
    for direction in range(3):
        stride = extent ** direction
        forward_half = space_shift(project(current, direction, -1.0), stride, extent, True)
        summed = summed + rebuild(colour_mul(gauge[direction], forward_half, False), direction, -1.0)
        behind = colour_mul(gauge[direction], project(current, direction, 1.0), True)
        summed = summed + rebuild(space_shift(behind, stride, extent, False), direction, 1.0)
    return summed


def chiral_sign(current):
    return jnp.concatenate([current[:, 0:2], -current[:, 2:4]], axis=1)


def fifth_term(current):
    count = current.shape[0]
    slice_index = jnp.arange(count).reshape(-1, 1, 1, 1, 1, 1)
    down_half = jnp.roll(current[:, 0:2], 1, axis=0) * jnp.where(slice_index == 0, -quark_mass, 1.0)
    up_half = jnp.roll(current[:, 2:4], -1, axis=0) * jnp.where(slice_index == count - 1, -quark_mass, 1.0)
    return jnp.concatenate([down_half, up_half], axis=1)


def dirac(current, gauge):
    hop_sum = space_hops(current, gauge, L)
    count = current.shape[-2]
    time_index = jnp.arange(count).reshape(-1, 1)
    forward_half = jnp.roll(project(current, 3, -1.0), -1, axis=-2) * jnp.where(time_index == count - 1, -1.0, 1.0)
    hop_sum = hop_sum + rebuild(colour_mul(gauge[3], forward_half, False), 3, -1.0)
    behind = jnp.roll(colour_mul(gauge[3], project(current, 3, 1.0), True), 1, axis=-2) * jnp.where(time_index == 0, -1.0, 1.0)
    hop_sum = hop_sum + rebuild(behind, 3, 1.0)
    return (5.0 - wall_height) * current - 0.5 * hop_sum - fifth_term(current)


def apply_hermitian(current, gauge):
    return jnp.flip(chiral_sign(dirac(current, gauge)), axis=0)


def reference(spinor, gauge_links):
    current = spinor.reshape(L5, 4, 3, 2, NT, SITES)
    gauge = gauge_links.reshape(4, 3, 3, 2, NT, SITES)
    previous = current
    current = (apply_hermitian(previous, gauge) - filter_center * previous) / filter_radius
    for order in range(1, DEGREE):
        following = 2.0 * (apply_hermitian(current, gauge) - filter_center * current) / filter_radius - previous
        previous, current = current, following
    return current.reshape(L5, 24, NT, SITES)
```

```python
import jax
import jax.numpy as jnp
import numpy as np
from jax import lax
from jax.experimental import pallas as pl
from jax.experimental.pallas import tpu as pltpu
from jax.sharding import PartitionSpec as P

DEGREE = 4
LANES = 128

wall_height = 1.8
quark_mass = 0.1
filter_center = 0.5
filter_radius = 8.0
gamma_block = (((1, 1), (0, 1)), ((1, 2), (0, 0)), ((0, 1), (1, 3)), ((0, 0), (1, 0)))
gamma_adjoint = (((1, 3), (0, 3)), ((1, 0), (0, 2)), ((0, 3), (1, 1)), ((0, 0), (1, 0)))
TIME = 3


def power_coefficients(degree):
    series = np.polynomial.chebyshev.cheb2poly([0.0] * degree + [1.0])
    line = np.polynomial.Polynomial([-filter_center / filter_radius, 1.0 / filter_radius])
    total = np.polynomial.Polynomial([0.0])
    for order, weight in enumerate(series):
        total = total + weight * line**order
    return [float(value) for value in total.coef]


def plus_unit(base, other, quarter, parity):
    turn = (quarter + (2 if parity < 0 else 0)) % 4
    if turn == 0:
        return base[0] + other[0], base[1] + other[1]
    if turn == 1:
        return base[0] - other[1], base[1] + other[0]
    if turn == 2:
        return base[0] - other[0], base[1] - other[1]
    return base[0] + other[1], base[1] - other[0]


def project(field, direction, parity):
    halves = []
    for row in range(2):
        source, quarter = gamma_block[direction][row]
        halves.append(
            [plus_unit(field[row][c], field[2 + source][c], quarter, parity) for c in range(3)]
        )
    return halves


def add_rebuilt(total, half, direction, parity):
    for row in range(2):
        source, quarter = gamma_adjoint[direction][row]
        for c in range(3):
            total[row][c] = (total[row][c][0] + half[row][c][0], total[row][c][1] + half[row][c][1])
            total[2 + row][c] = plus_unit(total[2 + row][c], half[source][c], quarter, parity)


def colour_mul(link, half, dagger):
    result = []
    for spin in range(2):
        rows = []
        for row in range(3):
            total = None
            for column in range(3):
                h_re, h_im = half[spin][column]
                if dagger:
                    l_re, l_im = link[column][row]
                    t_re = l_re * h_re + l_im * h_im
                    t_im = l_re * h_im - l_im * h_re
                else:
                    l_re, l_im = link[row][column]
                    t_re = l_re * h_re - l_im * h_im
                    t_im = l_re * h_im + l_im * h_re
                total = (t_re, t_im) if total is None else (total[0] + t_re, total[1] + t_im)
            rows.append(total)
        result.append(rows)
    return result


class Shape:
    def __init__(self, slices, sites):
        self.slices = slices
        self.sites = sites
        self.blocks = sites // LANES
        self.rows = slices * self.blocks
        self.extent = round(sites ** (1.0 / 3.0))
        assert self.extent**3 == sites and sites % LANES == 0


def index_of(shape, axis):
    return lax.broadcasted_iota(jnp.int32, (shape.rows, LANES), axis)


def turned(value, steps, axis):
    size = value.shape[axis]
    if steps % size == 0:
        return value
    return pltpu.roll(value, (-steps) % size, axis)


def space_shift(shape, stride, forward):
    extent = shape.extent
    group = stride * extent
    sign = 1 if forward else -1
    lane = index_of(shape, 1)
    if LANES % group == 0:
        place = lane // stride % extent
        edge = place == (extent - 1 if forward else 0)
        return lambda v: jnp.where(
            edge, turned(v, -sign * (extent - 1) * stride, 1), turned(v, sign * stride, 1)
        )
    assert group == shape.sites and stride < LANES
    block = index_of(shape, 0) % shape.blocks
    wraps = block == (shape.blocks - 1 if forward else 0)
    stays = lane < LANES - stride if forward else lane >= stride

    def shift(v):
        across = turned(v, sign * stride, 1)
        other = jnp.where(
            wraps, turned(across, -sign * (shape.blocks - 1), 0), turned(across, sign, 0)
        )
        return jnp.where(stays, across, other)

    return shift


def load_field(ref):
    return [[(ref[(s * 3 + c) * 2], ref[(s * 3 + c) * 2 + 1]) for c in range(3)] for s in range(4)]


def load_half(ref):
    return [[(ref[(s * 3 + c) * 2], ref[(s * 3 + c) * 2 + 1]) for c in range(3)] for s in range(2)]


def store_parts(ref, parts, rows=None):
    for s, colours in enumerate(parts):
        for c, pair in enumerate(colours):
            for p, value in enumerate(pair):
                if rows is None:
                    ref[(s * 3 + c) * 2 + p] = value
                else:
                    ref[(s * 3 + c) * 2 + p] = value[rows[0] : rows[1]]


def load_link(ref, direction):
    return [
        [(ref[direction * 18 + (r * 3 + c) * 2], ref[direction * 18 + (r * 3 + c) * 2 + 1]) for c in range(3)]
        for r in range(3)
    ]


def raw_field(shape, ref, mirrored):
    order = range(shape.slices)
    if mirrored:
        order = reversed(order)
    order = list(order)

    def part(index):
        return jnp.concatenate([ref[j, index] for j in order], axis=0)

    return [[(part((s * 3 + c) * 2), part((s * 3 + c) * 2 + 1)) for c in range(3)] for s in range(4)]


def pick(flag, first, second):
    return [
        [tuple(jnp.where(flag, a, b) for a, b in zip(p, q)) for p, q in zip(x, y)]
        for x, y in zip(first, second)
    ]


def send_parts(shape, field, link, even, odd_step, near_ref, far_ref, up_ref, down_ref):
    ahead = project(field, TIME, -1.0)
    behind = colour_mul(link, project(field, TIME, 1.0), True)
    store_parts(far_ref, pick(even, ahead, behind))
    first = (0, shape.blocks)
    last = (shape.rows - shape.blocks, shape.rows)
    upper, lower = field[0:2], field[2:4]
    store_parts(up_ref, lower if odd_step else upper, last)
    store_parts(down_ref, upper if odd_step else lower, first)
    store_parts(near_ref, pick(even, behind, ahead))


def widen_kernel(shape, links_ref, wide_ref):
    for mu in range(4):
        for index in range(18):
            value = links_ref[mu, index]
            wide_ref[mu * 18 + index] = jnp.concatenate([value] * shape.slices, axis=0)


def first_kernel(shape, scalar_ref, spinor_ref, links_ref, field_ref, near_ref, far_ref, up_ref, down_ref):
    even = scalar_ref[4] > 0.5
    field = raw_field(shape, spinor_ref, False)
    store_parts(field_ref, field)

    def link_part(index):
        return jnp.concatenate([links_ref[TIME, index]] * shape.slices, axis=0)

    link = [[(link_part((r * 3 + c) * 2), link_part((r * 3 + c) * 2 + 1)) for c in range(3)] for r in range(3)]
    send_parts(shape, field, link, even, False, near_ref, far_ref, up_ref, down_ref)


def space_kernel(shape, odd_step, field_ref, wide_ref, part_ref):
    field = load_field(field_ref)
    zero = jnp.zeros((shape.rows, LANES), jnp.float32)
    total = [[(zero, zero) for _ in range(3)] for _ in range(4)]
    for mu in range(3):
        stride = shape.extent**mu
        link = load_link(wide_ref, mu)
        ahead = space_shift(shape, stride, True)
        half = project(field, mu, -1.0)
        half = [[tuple(ahead(v) for v in pair) for pair in spin] for spin in half]
        add_rebuilt(total, colour_mul(link, half, False), mu, -1.0)
        behind = space_shift(shape, stride, False)
        half = colour_mul(link, project(field, mu, 1.0), True)
        half = [[tuple(behind(v) for v in pair) for pair in spin] for spin in half]
        add_rebuilt(total, half, mu, 1.0)
    row = index_of(shape, 0)
    inner_low = row >= shape.blocks
    inner_high = row < shape.rows - shape.blocks
    result = []
    for s in range(4):
        from_low = (s < 2) != odd_step
        colours = []
        for c in range(3):
            pair = []
            for p in range(2):
                value = field[s][c][p]
                if from_low:
                    hop = jnp.where(inner_low, turned(value, -shape.blocks, 0), 0.0)
                else:
                    hop = jnp.where(inner_high, turned(value, shape.blocks, 0), 0.0)
                pair.append((5.0 - wall_height) * value - 0.5 * total[s][c][p] - hop)
            colours.append(tuple(pair))
        result.append(colours)
    store_parts(part_ref, result)


def close_kernel(
    shape, odd_step, scale, weight, mirrored, last, scalar_ref, part_ref, wide_ref, start_ref, near_ref, far_ref,
    low_ref, high_ref, *out_refs
):
    even = scalar_ref[4] > 0.5
    low_sign, high_sign = scalar_ref[0], scalar_ref[1]
    low_mass, high_mass = scalar_ref[2], scalar_ref[3]
    link = load_link(wide_ref, TIME)
    near, far = load_half(near_ref), load_half(far_ref)
    ahead = colour_mul(link, pick(even, near, far), False)
    behind = pick(even, far, near)
    zero = jnp.zeros((shape.rows, LANES), jnp.float32)
    total = [[(zero, zero) for _ in range(3)] for _ in range(4)]
    ahead = [[tuple(v * high_sign for v in pair) for pair in spin] for spin in ahead]
    behind = [[tuple(v * low_sign for v in pair) for pair in spin] for spin in behind]
    add_rebuilt(total, ahead, TIME, -1.0)
    add_rebuilt(total, behind, TIME, 1.0)
    start = raw_field(shape, start_ref, mirrored)
    rest = jnp.zeros((shape.rows - shape.blocks, LANES), jnp.float32)
    field = []
    for s in range(4):
        from_low = (s < 2) != odd_step
        sign = scale if s < 2 else -scale
        colours = []
        for c in range(3):
            pair = []
            for p in range(2):
                index = (s * 3 + c) * 2 + p
                half_index = (s % 2 * 3 + c) * 2 + p
                if from_low:
                    hop = jnp.concatenate([low_ref[half_index] * low_mass, rest], axis=0)
                else:
                    hop = jnp.concatenate([rest, high_ref[half_index] * high_mass], axis=0)
                value = part_ref[index] - 0.5 * total[s][c][p] - hop
                pair.append(weight * start[s][c][p] + sign * value)
            colours.append(tuple(pair))
        field.append(colours)
    if last:
        (out_ref,) = out_refs
        for s in range(4):
            for c in range(3):
                for p in range(2):
                    for j in range(shape.slices):
                        out_ref[j, (s * 3 + c) * 2 + p] = field[s][c][p][j * shape.blocks : (j + 1) * shape.blocks]
        return
    field_ref, near_out, far_out, up_ref, down_ref = out_refs
    send_parts(shape, field, link, even, not odd_step, near_out, far_out, up_ref, down_ref)
    store_parts(field_ref, field)


def on_device(spinor, gauge_links):
    slices, _, depth, sites = spinor.shape
    assert depth == 1 and DEGREE % 2 == 0
    shape = Shape(slices, sites)
    rows, blocks = shape.rows, shape.blocks
    space_count = lax.axis_size("space")
    fifth_count = lax.axis_size("fifth")
    assert space_count % 2 == 0
    space_place = lax.axis_index("space")
    fifth_place = lax.axis_index("fifth")
    scalars = jnp.stack(
        [
            jnp.where(space_place == 0, -1.0, 1.0),
            jnp.where(space_place == space_count - 1, -1.0, 1.0),
            jnp.where(fifth_place == 0, -quark_mass, 1.0),
            jnp.where(fifth_place == fifth_count - 1, -quark_mass, 1.0),
            jnp.where(space_place % 2 == 0, 1.0, 0.0),
        ]
    ).astype(jnp.float32)
    near_pairs = [(i, i ^ 1) for i in range(space_count)]
    far_pairs = [(i, (i + (1 if i % 2 else -1)) % space_count) for i in range(space_count)]
    up_pairs = [(i, (i + 1) % fifth_count) for i in range(fifth_count)]
    down_pairs = [(i, (i - 1) % fifth_count) for i in range(fifth_count)]
    mirror_pairs = [(i, fifth_count - 1 - i) for i in range(fifth_count)]

    smem = pl.BlockSpec(memory_space=pltpu.SMEM)
    vmem = pl.BlockSpec(memory_space=pltpu.VMEM)

    def array(*dims):
        return jax.ShapeDtypeStruct(dims, jnp.float32)

    def call(body, out_shape, *operands, with_scalars):
        specs = ([smem] if with_scalars else []) + [vmem] * (len(operands) - with_scalars)
        return pl.pallas_call(
            body,
            out_shape=out_shape,
            in_specs=specs,
            out_specs=jax.tree.map(lambda _: vmem, out_shape),
        )(*operands)

    sends = (array(24, rows, LANES), array(12, rows, LANES), array(12, rows, LANES), array(12, blocks, LANES), array(12, blocks, LANES))
    weights = power_coefficients(DEGREE)

    start = spinor.reshape(slices, 24, blocks, LANES)
    links = gauge_links.reshape(4, 18, blocks, LANES)
    mirrored_start = lax.ppermute(start, "fifth", mirror_pairs)
    field, near, far, up, down = call(
        lambda *refs: first_kernel(shape, *refs), sends, scalars, start, links, with_scalars=1
    )
    wide = None
    for step in range(DEGREE):
        odd_step = step % 2 == 1
        far_in = lax.ppermute(far, "space", far_pairs)
        low_in = lax.ppermute(up, "fifth", up_pairs)
        high_in = lax.ppermute(down, "fifth", down_pairs)
        near_in = lax.ppermute(near, "space", near_pairs)
        if wide is None:
            wide = call(lambda *refs: widen_kernel(shape, *refs), array(72, rows, LANES), links, with_scalars=0)
        part = call(
            lambda *refs, odd_step=odd_step: space_kernel(shape, odd_step, *refs),
            array(24, rows, LANES), field, wide, with_scalars=0,
        )
        last = step == DEGREE - 1
        body = lambda *refs, odd_step=odd_step, step=step, last=last: close_kernel(
            shape, odd_step, weights[DEGREE] if step == 0 else 1.0, weights[DEGREE - 1 - step], not odd_step, last, *refs
        )
        result = call(
            body, array(slices, 24, blocks, LANES) if last else sends,
            scalars, part, wide, start if odd_step else mirrored_start, near_in, far_in, low_in, high_in,
            with_scalars=1,
        )
        if not last:
            field, near, far, up, down = result
    return result.reshape(slices, 24, depth, sites)


def solution(mesh):
    placed = (P("fifth", None, "space", None), P(None, None, "space", None))
    return jax.shard_map(
        on_device,
        mesh=mesh,
        in_specs=placed,
        out_specs=P("fifth", None, "space", None),
        check_vma=False,
    )
```

```python
import jax
import jax.numpy as jnp
import numpy as np
from jax import lax
from jax.experimental import pallas as pl
from jax.experimental.pallas import tpu as pltpu
from jax.sharding import PartitionSpec as P

DEGREE = 4
LANES = 128
VMEM_GRANT = 8 * 2**20

wall_height = 1.8
quark_mass = 0.1
filter_center = 0.5
filter_radius = 8.0
gamma_block = (((1, 1), (0, 1)), ((1, 2), (0, 0)), ((0, 1), (1, 3)), ((0, 0), (1, 0)))
gamma_adjoint = (((1, 3), (0, 3)), ((1, 0), (0, 2)), ((0, 3), (1, 1)), ((0, 0), (1, 0)))
TIME = 3


def power_coefficients(degree):
    series = np.polynomial.chebyshev.cheb2poly([0.0] * degree + [1.0])
    line = np.polynomial.Polynomial([-filter_center / filter_radius, 1.0 / filter_radius])
    total = np.polynomial.Polynomial([0.0])
    for order, weight in enumerate(series):
        total = total + weight * line**order
    return [float(value) for value in total.coef]


def plus_unit(base, other, quarter, parity):
    turn = (quarter + (2 if parity < 0 else 0)) % 4
    if turn == 0:
        return base[0] + other[0], base[1] + other[1]
    if turn == 1:
        return base[0] - other[1], base[1] + other[0]
    if turn == 2:
        return base[0] - other[0], base[1] - other[1]
    return base[0] + other[1], base[1] - other[0]


def project(field, direction, parity):
    halves = []
    for row in range(2):
        source, quarter = gamma_block[direction][row]
        halves.append(
            [plus_unit(field[row][c], field[2 + source][c], quarter, parity) for c in range(3)]
        )
    return halves


def add_rebuilt(total, half, direction, parity):
    for row in range(2):
        source, quarter = gamma_adjoint[direction][row]
        for c in range(3):
            total[row][c] = (total[row][c][0] + half[row][c][0], total[row][c][1] + half[row][c][1])
            total[2 + row][c] = plus_unit(total[2 + row][c], half[source][c], quarter, parity)


def colour_mul(link, half, dagger):
    result = []
    for spin in range(2):
        rows = []
        for row in range(3):
            total = None
            for column in range(3):
                h_re, h_im = half[spin][column]
                if dagger:
                    l_re, l_im = link[column][row]
                    t_re = l_re * h_re + l_im * h_im
                    t_im = l_re * h_im - l_im * h_re
                else:
                    l_re, l_im = link[row][column]
                    t_re = l_re * h_re - l_im * h_im
                    t_im = l_re * h_im + l_im * h_re
                total = (t_re, t_im) if total is None else (total[0] + t_re, total[1] + t_im)
            rows.append(total)
        result.append(rows)
    return result


class Shape:
    def __init__(self, slices, sites):
        self.slices = slices
        self.sites = sites
        self.blocks = sites // LANES
        self.rows = slices * self.blocks
        self.extent = round(sites ** (1.0 / 3.0))
        assert self.extent**3 == sites and sites % LANES == 0


def index_of(shape, axis):
    return lax.broadcasted_iota(jnp.int32, (shape.rows, LANES), axis)


def turned(value, steps, axis):
    size = value.shape[axis]
    if steps % size == 0:
        return value
    return pltpu.roll(value, (-steps) % size, axis)


def space_shift(shape, stride, forward):
    extent = shape.extent
    group = stride * extent
    sign = 1 if forward else -1
    lane = index_of(shape, 1)
    if LANES % group == 0:
        place = lane // stride % extent
        edge = place == (extent - 1 if forward else 0)
        return lambda v: jnp.where(
            edge, turned(v, -sign * (extent - 1) * stride, 1), turned(v, sign * stride, 1)
        )
    assert group == shape.sites and stride < LANES
    block = index_of(shape, 0) % shape.blocks
    wraps = block == (shape.blocks - 1 if forward else 0)
    stays = lane < LANES - stride if forward else lane >= stride

    def shift(v):
        across = turned(v, sign * stride, 1)
        other = jnp.where(
            wraps, turned(across, -sign * (shape.blocks - 1), 0), turned(across, sign, 0)
        )
        return jnp.where(stays, across, other)

    return shift


def load_field(ref):
    return [[(ref[(s * 3 + c) * 2], ref[(s * 3 + c) * 2 + 1]) for c in range(3)] for s in range(4)]


def load_half(ref):
    return [[(ref[(s * 3 + c) * 2], ref[(s * 3 + c) * 2 + 1]) for c in range(3)] for s in range(2)]


def store_parts(ref, parts, rows=None):
    for s, colours in enumerate(parts):
        for c, pair in enumerate(colours):
            for p, value in enumerate(pair):
                if rows is None:
                    ref[(s * 3 + c) * 2 + p] = value
                else:
                    ref[(s * 3 + c) * 2 + p] = value[rows[0] : rows[1]]


def load_link(ref, direction):
    return [
        [(ref[direction * 18 + (r * 3 + c) * 2], ref[direction * 18 + (r * 3 + c) * 2 + 1]) for c in range(3)]
        for r in range(3)
    ]


def raw_field(shape, ref, mirrored):
    order = range(shape.slices)
    if mirrored:
        order = reversed(order)
    order = list(order)

    def part(index):
        return jnp.concatenate([ref[j, index] for j in order], axis=0)

    return [[(part((s * 3 + c) * 2), part((s * 3 + c) * 2 + 1)) for c in range(3)] for s in range(4)]


def pick(flag, first, second):
    return [
        [tuple(jnp.where(flag, a, b) for a, b in zip(p, q)) for p, q in zip(x, y)]
        for x, y in zip(first, second)
    ]


class Place:
    def __init__(self):
        space, fifth = lax.axis_index("space"), lax.axis_index("fifth")
        last_space, last_fifth = lax.axis_size("space") - 1, lax.axis_size("fifth") - 1
        self.even = space % 2 == 0
        self.low_sign = jnp.where(space == 0, -1.0, 1.0)
        self.high_sign = jnp.where(space == last_space, -1.0, 1.0)
        self.low_mass = jnp.where(fifth == 0, -quark_mass, 1.0)
        self.high_mass = jnp.where(fifth == last_fifth, -quark_mass, 1.0)


def send_parts(shape, field, link, even, odd_step, near_ref, far_ref, up_ref, down_ref):
    ahead = project(field, TIME, -1.0)
    behind = colour_mul(link, project(field, TIME, 1.0), True)
    store_parts(far_ref, pick(even, ahead, behind))
    first = (0, shape.blocks)
    last = (shape.rows - shape.blocks, shape.rows)
    upper, lower = field[0:2], field[2:4]
    store_parts(up_ref, lower if odd_step else upper, last)
    store_parts(down_ref, upper if odd_step else lower, first)
    store_parts(near_ref, pick(even, behind, ahead))


def widen_kernel(shape, links_ref, wide_ref):
    for mu in range(4):
        for index in range(18):
            value = links_ref[mu, index]
            wide_ref[mu * 18 + index] = jnp.concatenate([value] * shape.slices, axis=0)


def first_kernel(shape, spinor_ref, links_ref, field_ref, near_ref, far_ref, up_ref, down_ref):
    even = Place().even
    field = raw_field(shape, spinor_ref, False)
    store_parts(field_ref, field)

    def link_part(index):
        return jnp.concatenate([links_ref[TIME, index]] * shape.slices, axis=0)

    link = [[(link_part((r * 3 + c) * 2), link_part((r * 3 + c) * 2 + 1)) for c in range(3)] for r in range(3)]
    send_parts(shape, field, link, even, False, near_ref, far_ref, up_ref, down_ref)


def space_kernel(shape, odd_step, field_ref, wide_ref, part_ref):
    field = load_field(field_ref)
    zero = jnp.zeros((shape.rows, LANES), jnp.float32)
    total = [[(zero, zero) for _ in range(3)] for _ in range(4)]
    for mu in range(3):
        stride = shape.extent**mu
        link = load_link(wide_ref, mu)
        ahead = space_shift(shape, stride, True)
        half = project(field, mu, -1.0)
        half = [[tuple(ahead(v) for v in pair) for pair in spin] for spin in half]
        add_rebuilt(total, colour_mul(link, half, False), mu, -1.0)
        behind = space_shift(shape, stride, False)
        half = colour_mul(link, project(field, mu, 1.0), True)
        half = [[tuple(behind(v) for v in pair) for pair in spin] for spin in half]
        add_rebuilt(total, half, mu, 1.0)
    row = index_of(shape, 0)
    inner_low = row >= shape.blocks
    inner_high = row < shape.rows - shape.blocks
    result = []
    for s in range(4):
        from_low = (s < 2) != odd_step
        colours = []
        for c in range(3):
            pair = []
            for p in range(2):
                value = field[s][c][p]
                if from_low:
                    hop = jnp.where(inner_low, turned(value, -shape.blocks, 0), 0.0)
                else:
                    hop = jnp.where(inner_high, turned(value, shape.blocks, 0), 0.0)
                pair.append((5.0 - wall_height) * value - 0.5 * total[s][c][p] - hop)
            colours.append(tuple(pair))
        result.append(colours)
    store_parts(part_ref, result)


def close_kernel(
    shape, odd_step, scale, weight, mirrored, last, part_ref, wide_ref, start_ref, near_ref, far_ref,
    low_ref, high_ref, *out_refs
):
    place = Place()
    even = place.even
    link = load_link(wide_ref, TIME)
    near, far = load_half(near_ref), load_half(far_ref)
    ahead = colour_mul(link, pick(even, near, far), False)
    behind = pick(even, far, near)
    zero = jnp.zeros((shape.rows, LANES), jnp.float32)
    total = [[(zero, zero) for _ in range(3)] for _ in range(4)]
    ahead = [[tuple(v * place.high_sign for v in pair) for pair in spin] for spin in ahead]
    behind = [[tuple(v * place.low_sign for v in pair) for pair in spin] for spin in behind]
    add_rebuilt(total, ahead, TIME, -1.0)
    add_rebuilt(total, behind, TIME, 1.0)
    start = raw_field(shape, start_ref, mirrored)
    rest = jnp.zeros((shape.rows - shape.blocks, LANES), jnp.float32)
    field = []
    for s in range(4):
        from_low = (s < 2) != odd_step
        sign = scale if s < 2 else -scale
        colours = []
        for c in range(3):
            pair = []
            for p in range(2):
                index = (s * 3 + c) * 2 + p
                half_index = (s % 2 * 3 + c) * 2 + p
                if from_low:
                    hop = jnp.concatenate([low_ref[half_index] * place.low_mass, rest], axis=0)
                else:
                    hop = jnp.concatenate([rest, high_ref[half_index] * place.high_mass], axis=0)
                value = part_ref[index] - 0.5 * total[s][c][p] - hop
                pair.append(weight * start[s][c][p] + sign * value)
            colours.append(tuple(pair))
        field.append(colours)
    if last:
        (out_ref,) = out_refs
        for s in range(4):
            for c in range(3):
                for p in range(2):
                    for j in range(shape.slices):
                        out_ref[j, (s * 3 + c) * 2 + p] = field[s][c][p][j * shape.blocks : (j + 1) * shape.blocks]
        return
    field_ref, near_out, far_out, up_ref, down_ref = out_refs
    send_parts(shape, field, link, even, not odd_step, near_out, far_out, up_ref, down_ref)
    store_parts(field_ref, field)


def on_device(spinor, gauge_links):
    slices, _, depth, sites = spinor.shape
    assert depth == 1 and DEGREE % 2 == 0
    shape = Shape(slices, sites)
    rows, blocks = shape.rows, shape.blocks
    space_count = lax.axis_size("space")
    fifth_count = lax.axis_size("fifth")
    assert space_count % 2 == 0
    near_pairs = [(i, i ^ 1) for i in range(space_count)]
    far_pairs = [(i, (i + (1 if i % 2 else -1)) % space_count) for i in range(space_count)]
    up_pairs = [(i, (i + 1) % fifth_count) for i in range(fifth_count)]
    down_pairs = [(i, (i - 1) % fifth_count) for i in range(fifth_count)]
    mirror_pairs = [(i, fifth_count - 1 - i) for i in range(fifth_count)]

    vmem = pl.BlockSpec(memory_space=pltpu.VMEM)

    def array(*dims):
        return jax.ShapeDtypeStruct(dims, jnp.float32)

    def call(body, out_shape, *operands):
        return pl.pallas_call(
            body,
            out_shape=out_shape,
            in_specs=[vmem] * len(operands),
            out_specs=jax.tree.map(lambda _: vmem, out_shape),
            compiler_params=pltpu.CompilerParams(vmem_limit_bytes=VMEM_GRANT),
        )(*operands)

    sends = (array(24, rows, LANES), array(12, rows, LANES), array(12, rows, LANES), array(12, blocks, LANES), array(12, blocks, LANES))
    weights = power_coefficients(DEGREE)

    start = spinor.reshape(slices, 24, blocks, LANES)
    links = gauge_links.reshape(4, 18, blocks, LANES)
    mirrored_start = lax.ppermute(start, "fifth", mirror_pairs)
    field, near, far, up, down = call(
        lambda *refs: first_kernel(shape, *refs), sends, start, links
    )
    wide = None
    for step in range(DEGREE):
        odd_step = step % 2 == 1
        far_in = lax.ppermute(far, "space", far_pairs)
        low_in = lax.ppermute(up, "fifth", up_pairs)
        high_in = lax.ppermute(down, "fifth", down_pairs)
        near_in = lax.ppermute(near, "space", near_pairs)
        if wide is None:
            wide = call(lambda *refs: widen_kernel(shape, *refs), array(72, rows, LANES), links)
        part = call(
            lambda *refs, odd_step=odd_step: space_kernel(shape, odd_step, *refs),
            array(24, rows, LANES), field, wide,
        )
        last = step == DEGREE - 1
        body = lambda *refs, odd_step=odd_step, step=step, last=last: close_kernel(
            shape, odd_step, weights[DEGREE] if step == 0 else 1.0, weights[DEGREE - 1 - step], not odd_step, last, *refs
        )
        result = call(
            body, array(slices, 24, blocks, LANES) if last else sends,
            part, wide, start if odd_step else mirrored_start, near_in, far_in, low_in, high_in,
        )
        if not last:
            field, near, far, up, down = result
    return result.reshape(slices, 24, depth, sites)


def solution(mesh):
    placed = (P("fifth", None, "space", None), P(None, None, "space", None))
    return jax.shard_map(
        on_device,
        mesh=mesh,
        in_specs=placed,
        out_specs=P("fifth", None, "space", None),
        check_vma=False,
    )
```

```python
import jax
import jax.numpy as jnp
import numpy as np
from jax import lax
from jax.experimental import pallas as pl
from jax.experimental.pallas import tpu as pltpu
from jax.sharding import PartitionSpec as P

DEGREE = 4
LANES = 128
VMEM_GRANT = 8 * 2**20
TABLE_FLOPS = 10**8

wall_height = 1.8
quark_mass = 0.1
filter_center = 0.5
filter_radius = 8.0
gamma_block = (((1, 1), (0, 1)), ((1, 2), (0, 0)), ((0, 1), (1, 3)), ((0, 0), (1, 0)))
gamma_adjoint = (((1, 3), (0, 3)), ((1, 0), (0, 2)), ((0, 3), (1, 1)), ((0, 0), (1, 0)))
TIME = 3


def power_coefficients(degree):
    series = np.polynomial.chebyshev.cheb2poly([0.0] * degree + [1.0])
    line = np.polynomial.Polynomial([-filter_center / filter_radius, 1.0 / filter_radius])
    total = np.polynomial.Polynomial([0.0])
    for order, weight in enumerate(series):
        total = total + weight * line**order
    return [float(value) for value in total.coef]


def plus_unit(base, other, quarter, parity):
    turn = (quarter + (2 if parity < 0 else 0)) % 4
    if turn == 0:
        return base[0] + other[0], base[1] + other[1]
    if turn == 1:
        return base[0] - other[1], base[1] + other[0]
    if turn == 2:
        return base[0] - other[0], base[1] - other[1]
    return base[0] + other[1], base[1] - other[0]


def project(field, direction, parity):
    halves = []
    for row in range(2):
        source, quarter = gamma_block[direction][row]
        halves.append(
            [plus_unit(field[row][c], field[2 + source][c], quarter, parity) for c in range(3)]
        )
    return halves


def add_rebuilt(total, half, direction, parity):
    for row in range(2):
        source, quarter = gamma_adjoint[direction][row]
        for c in range(3):
            total[row][c] = (total[row][c][0] + half[row][c][0], total[row][c][1] + half[row][c][1])
            total[2 + row][c] = plus_unit(total[2 + row][c], half[source][c], quarter, parity)


def colour_mul(link, half, dagger):
    result = []
    for spin in range(2):
        rows = []
        for row in range(3):
            total = None
            for column in range(3):
                h_re, h_im = half[spin][column]
                if dagger:
                    l_re, l_im = link[column][row]
                    t_re = l_re * h_re + l_im * h_im
                    t_im = l_re * h_im - l_im * h_re
                else:
                    l_re, l_im = link[row][column]
                    t_re = l_re * h_re - l_im * h_im
                    t_im = l_re * h_im + l_im * h_re
                total = (t_re, t_im) if total is None else (total[0] + t_re, total[1] + t_im)
            rows.append(total)
        result.append(rows)
    return result


class Shape:
    def __init__(self, slices, sites):
        self.slices = slices
        self.sites = sites
        self.blocks = sites // LANES
        self.rows = slices * self.blocks
        self.extent = round(sites ** (1.0 / 3.0))
        assert self.extent**3 == sites and sites % LANES == 0


def index_of(shape, axis):
    return lax.broadcasted_iota(jnp.int32, (shape.rows, LANES), axis)


def turned(value, steps, axis):
    size = value.shape[axis]
    if steps % size == 0:
        return value
    return pltpu.roll(value, (-steps) % size, axis)


def space_shift(shape, stride, forward):
    extent = shape.extent
    group = stride * extent
    sign = 1 if forward else -1
    lane = index_of(shape, 1)
    if LANES % group == 0:
        place = lane // stride % extent
        edge = place == (extent - 1 if forward else 0)
        return lambda v: jnp.where(
            edge, turned(v, -sign * (extent - 1) * stride, 1), turned(v, sign * stride, 1)
        )
    assert group == shape.sites and stride < LANES
    block = index_of(shape, 0) % shape.blocks
    wraps = block == (shape.blocks - 1 if forward else 0)
    stays = lane < LANES - stride if forward else lane >= stride

    def shift(v):
        across = turned(v, sign * stride, 1)
        other = jnp.where(
            wraps, turned(across, -sign * (shape.blocks - 1), 0), turned(across, sign, 0)
        )
        return jnp.where(stays, across, other)

    return shift


def load_field(ref):
    return [[(ref[(s * 3 + c) * 2], ref[(s * 3 + c) * 2 + 1]) for c in range(3)] for s in range(4)]


def load_half(ref):
    return [[(ref[(s * 3 + c) * 2], ref[(s * 3 + c) * 2 + 1]) for c in range(3)] for s in range(2)]


def store_parts(ref, parts, rows=None):
    for s, colours in enumerate(parts):
        for c, pair in enumerate(colours):
            for p, value in enumerate(pair):
                if rows is None:
                    ref[(s * 3 + c) * 2 + p] = value
                else:
                    ref[(s * 3 + c) * 2 + p] = value[rows[0] : rows[1]]


def load_link(ref, direction):
    return [
        [(ref[direction * 18 + (r * 3 + c) * 2], ref[direction * 18 + (r * 3 + c) * 2 + 1]) for c in range(3)]
        for r in range(3)
    ]


def raw_field(shape, ref, mirrored):
    order = range(shape.slices)
    if mirrored:
        order = reversed(order)
    order = list(order)

    def part(index):
        return jnp.concatenate([ref[j, index] for j in order], axis=0)

    return [[(part((s * 3 + c) * 2), part((s * 3 + c) * 2 + 1)) for c in range(3)] for s in range(4)]


def cut(parts, low, high):
    return [[tuple(v[low:high] for v in pair) for pair in spin] for spin in parts]


def pick(flag, first, second):
    return [
        [tuple(jnp.where(flag, a, b) for a, b in zip(p, q)) for p, q in zip(x, y)]
        for x, y in zip(first, second)
    ]


class Place:
    def __init__(self):
        space, fifth = lax.axis_index("space"), lax.axis_index("fifth")
        last_space, last_fifth = lax.axis_size("space") - 1, lax.axis_size("fifth") - 1
        self.even = space % 2 == 0
        self.fifth_even = fifth % 2 == 0
        self.low_sign = jnp.where(space == 0, -1.0, 1.0)
        self.high_sign = jnp.where(space == last_space, -1.0, 1.0)
        self.low_mass = jnp.where(fifth == 0, -quark_mass, 1.0)
        self.high_mass = jnp.where(fifth == last_fifth, -quark_mass, 1.0)


def send_parts(shape, field, link, place, odd_step, near_ref, far_ref, side_ref, across_ref):
    ahead = project(field, TIME, -1.0)
    behind = colour_mul(link, project(field, TIME, 1.0), True)
    store_parts(far_ref, pick(place.even, ahead, behind))
    upper, lower = field[0:2], field[2:4]
    up = cut(lower if odd_step else upper, shape.rows - shape.blocks, shape.rows)
    down = cut(upper if odd_step else lower, 0, shape.blocks)
    if across_ref is not None:
        store_parts(across_ref, pick(place.fifth_even, down, up))
    store_parts(side_ref, pick(place.fifth_even, up, down))
    store_parts(near_ref, pick(place.even, behind, ahead))


def widen_kernel(shape, links_ref, wide_ref):
    for mu in range(4):
        for index in range(18):
            value = links_ref[mu, index]
            wide_ref[mu * 18 + index] = jnp.concatenate([value] * shape.slices, axis=0)


def table_kernel(table_ref):
    place = Place()
    even = jnp.where(place.even, 1.0, 0.0)
    values = (even, place.low_sign, place.high_sign, place.low_mass, place.high_mass)
    for row, value in enumerate(values):
        table_ref[row : row + 1] = jnp.full((1, LANES), value, jnp.float32)
    table_ref[len(values) :] = jnp.zeros((8 - len(values), LANES), jnp.float32)


def first_kernel(shape, spinor_ref, links_ref, table_ref, field_ref, near_ref, far_ref, side_ref, across_ref, link_ref, sems):
    copies = []
    for j in range(shape.slices):
        part = pl.ds(j * shape.blocks, shape.blocks)
        copies.append((spinor_ref.at[j], field_ref.at[:, part]))
        copies.append((links_ref.at[TIME], link_ref.at[:, part]))
    copies = [pltpu.make_async_copy(a, b, sems.at[i]) for i, (a, b) in enumerate(copies)]
    for copy in copies:
        copy.start()
    for copy in copies:
        copy.wait()
    place = Place()
    place.even = table_ref[0:1] > 0.5
    field, link = load_field(field_ref), load_link(link_ref, 0)
    send_parts(shape, field, link, place, False, near_ref, far_ref, side_ref, across_ref)


def space_kernel(shape, odd_step, field_ref, wide_ref, part_ref):
    field = load_field(field_ref)
    zero = jnp.zeros((shape.rows, LANES), jnp.float32)
    total = [[(zero, zero) for _ in range(3)] for _ in range(4)]
    for mu in range(3):
        stride = shape.extent**mu
        link = load_link(wide_ref, mu)
        ahead = space_shift(shape, stride, True)
        half = project(field, mu, -1.0)
        half = [[tuple(ahead(v) for v in pair) for pair in spin] for spin in half]
        add_rebuilt(total, colour_mul(link, half, False), mu, -1.0)
        behind = space_shift(shape, stride, False)
        half = colour_mul(link, project(field, mu, 1.0), True)
        half = [[tuple(behind(v) for v in pair) for pair in spin] for spin in half]
        add_rebuilt(total, half, mu, 1.0)
    row = index_of(shape, 0)
    inner_low = row >= shape.blocks
    inner_high = row < shape.rows - shape.blocks
    result = []
    for s in range(4):
        from_low = (s < 2) != odd_step
        colours = []
        for c in range(3):
            pair = []
            for p in range(2):
                value = field[s][c][p]
                if from_low:
                    hop = jnp.where(inner_low, turned(value, -shape.blocks, 0), 0.0)
                else:
                    hop = jnp.where(inner_high, turned(value, shape.blocks, 0), 0.0)
                pair.append((5.0 - wall_height) * value - 0.5 * total[s][c][p] - hop)
            colours.append(tuple(pair))
        result.append(colours)
    store_parts(part_ref, result)


def close_kernel(
    shape, odd_step, scale, weight, last, part_ref, wide_ref, start_ref, near_ref, far_ref, side_ref, across_ref, out_refs
):
    place = Place()
    even = place.even
    link = load_link(wide_ref, TIME)
    near, far = load_half(near_ref), load_half(far_ref)
    ahead = colour_mul(link, pick(even, near, far), False)
    behind = pick(even, far, near)
    zero = jnp.zeros((shape.rows, LANES), jnp.float32)
    total = [[(zero, zero) for _ in range(3)] for _ in range(4)]
    ahead = [[tuple(v * place.high_sign for v in pair) for pair in spin] for spin in ahead]
    behind = [[tuple(v * place.low_sign for v in pair) for pair in spin] for spin in behind]
    add_rebuilt(total, ahead, TIME, -1.0)
    add_rebuilt(total, behind, TIME, 1.0)
    start = load_field(start_ref) if odd_step else raw_field(shape, start_ref, True)
    side = load_half(side_ref)
    if across_ref is None:
        final = [[tuple(start_ref[shape.slices - 1, (s * 3 + c) * 2 + p] for p in range(2)) for c in range(3)] for s in range(2)]
        first = [[tuple(start_ref[0, (s * 3 + c) * 2 + p] for p in range(2)) for c in range(3)] for s in range(2, 4)]
        across = pick(place.fifth_even, final, first)
    else:
        across = load_half(across_ref)
    low = pick(place.fifth_even, across, side)
    high = pick(place.fifth_even, side, across)
    rest = jnp.zeros((shape.rows - shape.blocks, LANES), jnp.float32)
    field = []
    for s in range(4):
        from_low = (s < 2) != odd_step
        sign = scale if s < 2 else -scale
        colours = []
        for c in range(3):
            pair = []
            for p in range(2):
                index = (s * 3 + c) * 2 + p
                if from_low:
                    hop = jnp.concatenate([low[s % 2][c][p] * place.low_mass, rest], axis=0)
                else:
                    hop = jnp.concatenate([rest, high[s % 2][c][p] * place.high_mass], axis=0)
                value = part_ref[index] - 0.5 * total[s][c][p] - hop
                pair.append(weight * start[s][c][p] + sign * value)
            colours.append(tuple(pair))
        field.append(colours)
    if last:
        (out_ref,) = out_refs
        for s in range(4):
            for c in range(3):
                for p in range(2):
                    for j in range(shape.slices):
                        out_ref[j, (s * 3 + c) * 2 + p] = field[s][c][p][j * shape.blocks : (j + 1) * shape.blocks]
        return
    field_ref, near_out, far_out, side_out, across_out = out_refs
    send_parts(shape, field, link, place, not odd_step, near_out, far_out, side_out, across_out)
    store_parts(field_ref, field)


def on_device(spinor, gauge_links):
    slices, _, depth, sites = spinor.shape
    space_count = lax.axis_size("space")
    fifth_count = lax.axis_size("fifth")
    assert depth == 1 and DEGREE % 2 == 0 and space_count % 2 == 0 and fifth_count % 2 == 0
    shape = Shape(slices, sites)
    rows, blocks = shape.rows, shape.blocks
    near_pairs = [(i, i ^ 1) for i in range(space_count)]
    far_pairs = [(i, (i + (1 if i % 2 else -1)) % space_count) for i in range(space_count)]
    side_pairs = [(i, i ^ 1) for i in range(fifth_count)]
    across_pairs = [(i, (i + (1 if i % 2 else -1)) % fifth_count) for i in range(fifth_count)]
    mirror_pairs = [(i, fifth_count - 1 - i) for i in range(fifth_count)]
    first_across = across_pairs != mirror_pairs

    vmem = pl.BlockSpec(memory_space=pltpu.VMEM)
    hbm = pl.BlockSpec(memory_space=pltpu.HBM)

    def array(*dims):
        return jax.ShapeDtypeStruct(dims, jnp.float32)

    def call(body, out_shape, *operands, operand_specs=None, scratch=()):
        return pl.pallas_call(
            body,
            out_shape=out_shape,
            in_specs=operand_specs or [vmem] * len(operands),
            out_specs=jax.tree.map(lambda _: vmem, out_shape),
            scratch_shapes=scratch,
            compiler_params=pltpu.CompilerParams(vmem_limit_bytes=VMEM_GRANT),
        )(*operands)

    whole, half, edge = array(24, rows, LANES), array(12, rows, LANES), array(12, blocks, LANES)
    weights = power_coefficients(DEGREE)
    start = spinor.reshape(slices, 24, blocks, LANES)
    links = gauge_links.reshape(4, 18, blocks, LANES)
    table = pl.pallas_call(
        table_kernel,
        out_shape=array(8, LANES),
        out_specs=vmem,
        cost_estimate=pl.CostEstimate(flops=TABLE_FLOPS, bytes_accessed=4096, transcendentals=0),
        compiler_params=pltpu.CompilerParams(vmem_limit_bytes=VMEM_GRANT),
    )()
    mirrored = lax.ppermute(start, "fifth", mirror_pairs)

    def first(spinor_ref, links_ref, table_ref, field_ref, near_ref, far_ref, side_ref, *rest):
        across_ref = rest[0] if first_across else None
        first_kernel(shape, spinor_ref, links_ref, table_ref, field_ref, near_ref, far_ref, side_ref, across_ref, *rest[-2:])

    sends = (whole, half, half, edge) + ((edge,) if first_across else ())
    scratch = (pltpu.VMEM((18, rows, LANES), jnp.float32), pltpu.SemaphoreType.DMA((2 * slices,)))
    origin, near, far, side, *across = call(first, sends, start, links, table, operand_specs=(hbm, hbm, vmem), scratch=scratch)
    field, wide = origin, None
    for step in range(DEGREE):
        odd_step, last = step % 2 == 1, step == DEGREE - 1
        far_in = lax.ppermute(far, "space", far_pairs)
        across_in = [lax.ppermute(value, "fifth", across_pairs) for value in across]
        side_in = lax.ppermute(side, "fifth", side_pairs)
        near_in = lax.ppermute(near, "space", near_pairs)
        if wide is None:
            wide = call(lambda *refs: widen_kernel(shape, *refs), array(72, rows, LANES), links)
        part = call(lambda *refs, odd=odd_step: space_kernel(shape, odd, *refs), whole, field, wide)
        scale = weights[DEGREE] if step == 0 else 1.0

        def close(*refs, step=step, odd=odd_step, last=last, scale=scale, count=len(across)):
            across_ref = refs[6] if count else None
            close_kernel(shape, odd, scale, weights[DEGREE - 1 - step], last, *refs[:6], across_ref, refs[6 + count :])

        operands = (part, wide, origin if odd_step else mirrored, near_in, far_in, side_in, *across_in)
        if last:
            result = call(close, array(slices, 24, blocks, LANES), *operands)
        else:
            field, near, far, side, *across = call(close, (whole, half, half, edge, edge), *operands)
    return result.reshape(slices, 24, depth, sites)


def solution(mesh):
    placed = (P("fifth", None, "space", None), P(None, None, "space", None))
    return jax.shard_map(
        on_device,
        mesh=mesh,
        in_specs=placed,
        out_specs=P("fifth", None, "space", None),
        check_vma=False,
    )
```

```python
import jax
import jax.numpy as jnp
import numpy as np
from jax import lax
from jax.experimental import pallas as pl
from jax.experimental.pallas import tpu as pltpu
from jax.sharding import PartitionSpec as P

DEGREE = 4
LANES = 128
VMEM_GRANT = 8 * 2**20
TABLE_FLOPS = 10**8

wall_height = 1.8
quark_mass = 0.1
filter_center = 0.5
filter_radius = 8.0
gamma_block = (((1, 1), (0, 1)), ((1, 2), (0, 0)), ((0, 1), (1, 3)), ((0, 0), (1, 0)))
gamma_adjoint = (((1, 3), (0, 3)), ((1, 0), (0, 2)), ((0, 3), (1, 1)), ((0, 0), (1, 0)))
TIME = 3


def power_coefficients(degree):
    series = np.polynomial.chebyshev.cheb2poly([0.0] * degree + [1.0])
    line = np.polynomial.Polynomial([-filter_center / filter_radius, 1.0 / filter_radius])
    total = np.polynomial.Polynomial([0.0])
    for order, weight in enumerate(series):
        total = total + weight * line**order
    return [float(value) for value in total.coef]


def plus_unit(base, other, quarter, parity):
    turn = (quarter + (2 if parity < 0 else 0)) % 4
    if turn == 0:
        return base[0] + other[0], base[1] + other[1]
    if turn == 1:
        return base[0] - other[1], base[1] + other[0]
    if turn == 2:
        return base[0] - other[0], base[1] - other[1]
    return base[0] + other[1], base[1] - other[0]


def project(field, direction, parity):
    halves = []
    for row in range(2):
        source, quarter = gamma_block[direction][row]
        halves.append(
            [plus_unit(field[row][c], field[2 + source][c], quarter, parity) for c in range(3)]
        )
    return halves


def add_rebuilt(total, half, direction, parity):
    for row in range(2):
        source, quarter = gamma_adjoint[direction][row]
        for c in range(3):
            total[row][c] = (total[row][c][0] + half[row][c][0], total[row][c][1] + half[row][c][1])
            total[2 + row][c] = plus_unit(total[2 + row][c], half[source][c], quarter, parity)


def colour_mul(link, half, dagger):
    result = []
    for spin in range(2):
        rows = []
        for row in range(3):
            total = None
            for column in range(3):
                h_re, h_im = half[spin][column]
                if dagger:
                    l_re, l_im = link[column][row]
                    t_re = l_re * h_re + l_im * h_im
                    t_im = l_re * h_im - l_im * h_re
                else:
                    l_re, l_im = link[row][column]
                    t_re = l_re * h_re - l_im * h_im
                    t_im = l_re * h_im + l_im * h_re
                total = (t_re, t_im) if total is None else (total[0] + t_re, total[1] + t_im)
            rows.append(total)
        result.append(rows)
    return result


class Shape:
    def __init__(self, slices, sites):
        self.slices = slices
        self.sites = sites
        self.blocks = sites // LANES
        self.rows = slices * self.blocks
        self.extent = round(sites ** (1.0 / 3.0))
        assert self.extent**3 == sites and sites % LANES == 0


def index_of(shape, axis):
    return lax.broadcasted_iota(jnp.int32, (shape.rows, LANES), axis)


def turned(value, steps, axis):
    size = value.shape[axis]
    if steps % size == 0:
        return value
    return pltpu.roll(value, (-steps) % size, axis)


def space_shift(shape, stride, forward):
    extent = shape.extent
    group = stride * extent
    sign = 1 if forward else -1
    lane = index_of(shape, 1)
    if LANES % group == 0:
        place = lane // stride % extent
        edge = place == (extent - 1 if forward else 0)
        return lambda v: jnp.where(
            edge, turned(v, -sign * (extent - 1) * stride, 1), turned(v, sign * stride, 1)
        )
    assert group == shape.sites and stride < LANES
    block = index_of(shape, 0) % shape.blocks
    wraps = block == (shape.blocks - 1 if forward else 0)
    stays = lane < LANES - stride if forward else lane >= stride

    def shift(v):
        across = turned(v, sign * stride, 1)
        other = jnp.where(
            wraps, turned(across, -sign * (shape.blocks - 1), 0), turned(across, sign, 0)
        )
        return jnp.where(stays, across, other)

    return shift


def load_field(ref):
    return [[(ref[(s * 3 + c) * 2], ref[(s * 3 + c) * 2 + 1]) for c in range(3)] for s in range(4)]


def load_half(ref):
    return [[(ref[(s * 3 + c) * 2], ref[(s * 3 + c) * 2 + 1]) for c in range(3)] for s in range(2)]


def store_parts(ref, parts, rows=None):
    for s, colours in enumerate(parts):
        for c, pair in enumerate(colours):
            for p, value in enumerate(pair):
                if rows is None:
                    ref[(s * 3 + c) * 2 + p] = value
                else:
                    ref[(s * 3 + c) * 2 + p] = value[rows[0] : rows[1]]


def load_link(ref, direction):
    return [
        [(ref[direction * 18 + (r * 3 + c) * 2], ref[direction * 18 + (r * 3 + c) * 2 + 1]) for c in range(3)]
        for r in range(3)
    ]


def raw_field(shape, ref, mirrored):
    order = range(shape.slices)
    if mirrored:
        order = reversed(order)
    order = list(order)

    def part(index):
        return jnp.concatenate([ref[j, index] for j in order], axis=0)

    return [[(part((s * 3 + c) * 2), part((s * 3 + c) * 2 + 1)) for c in range(3)] for s in range(4)]


def cut(parts, low, high):
    return [[tuple(v[low:high] for v in pair) for pair in spin] for spin in parts]


def pick(flag, first, second):
    return [
        [tuple(jnp.where(flag, a, b) for a, b in zip(p, q)) for p, q in zip(x, y)]
        for x, y in zip(first, second)
    ]


class Place:
    def __init__(self):
        space, fifth = lax.axis_index("space"), lax.axis_index("fifth")
        last_space, last_fifth = lax.axis_size("space") - 1, lax.axis_size("fifth") - 1
        self.even = space % 2 == 0
        self.fifth_even = fifth % 2 == 0
        self.low_sign = jnp.where(space == 0, -1.0, 1.0)
        self.high_sign = jnp.where(space == last_space, -1.0, 1.0)
        self.low_mass = jnp.where(fifth == 0, -quark_mass, 1.0)
        self.high_mass = jnp.where(fifth == last_fifth, -quark_mass, 1.0)


def send_parts(shape, field, link, place, odd_step, near_ref, far_ref, side_ref, across_ref):
    ahead = project(field, TIME, -1.0)
    behind = colour_mul(link, project(field, TIME, 1.0), True)
    store_parts(far_ref, pick(place.even, ahead, behind))
    upper, lower = field[0:2], field[2:4]
    up = cut(lower if odd_step else upper, shape.rows - shape.blocks, shape.rows)
    down = cut(upper if odd_step else lower, 0, shape.blocks)
    if across_ref is not None:
        store_parts(across_ref, pick(place.fifth_even, down, up))
    store_parts(side_ref, pick(place.fifth_even, up, down))
    store_parts(near_ref, pick(place.even, behind, ahead))


def widen_kernel(shape, links_ref, wide_ref):
    for mu in range(4):
        for index in range(18):
            value = links_ref[mu, index]
            wide_ref[mu * 18 + index] = jnp.concatenate([value] * shape.slices, axis=0)


def table_kernel(table_ref):
    place = Place()
    even = jnp.where(place.even, 1.0, 0.0)
    values = (even, place.low_sign, place.high_sign, place.low_mass, place.high_mass)
    for row, value in enumerate(values):
        table_ref[row : row + 1] = jnp.full((1, LANES), value, jnp.float32)
    table_ref[len(values) :] = jnp.zeros((8 - len(values), LANES), jnp.float32)


def first_kernel(shape, spinor_ref, links_ref, table_ref, field_ref, near_ref, far_ref, side_ref, across_ref, link_ref, sems):
    copies = []
    for j in range(shape.slices):
        part = pl.ds(j * shape.blocks, shape.blocks)
        copies.append((spinor_ref.at[j], field_ref.at[:, part]))
        copies.append((links_ref.at[TIME], link_ref.at[:, part]))
    copies = [pltpu.make_async_copy(a, b, sems.at[i]) for i, (a, b) in enumerate(copies)]
    for copy in copies:
        copy.start()
    for copy in copies:
        copy.wait()
    place = Place()
    place.even = table_ref[0:1] > 0.5
    field, link = load_field(field_ref), load_link(link_ref, 0)
    send_parts(shape, field, link, place, False, near_ref, far_ref, side_ref, across_ref)


def space_hops(shape, field, wide_ref):
    zero = jnp.zeros((shape.rows, LANES), jnp.float32)
    total = [[(zero, zero) for _ in range(3)] for _ in range(4)]
    for mu in range(3):
        stride = shape.extent**mu
        link = load_link(wide_ref, mu)
        ahead = space_shift(shape, stride, True)
        half = project(field, mu, -1.0)
        half = [[tuple(ahead(v) for v in pair) for pair in spin] for spin in half]
        add_rebuilt(total, colour_mul(link, half, False), mu, -1.0)
        behind = space_shift(shape, stride, False)
        half = colour_mul(link, project(field, mu, 1.0), True)
        half = [[tuple(behind(v) for v in pair) for pair in spin] for spin in half]
        add_rebuilt(total, half, mu, 1.0)
    return total


def space_kernel(shape, odd_step, field_ref, wide_ref, part_ref):
    field = load_field(field_ref)
    total = space_hops(shape, field, wide_ref)
    row = index_of(shape, 0)
    inner_low = row >= shape.blocks
    inner_high = row < shape.rows - shape.blocks
    result = []
    for s in range(4):
        from_low = (s < 2) != odd_step
        colours = []
        for c in range(3):
            pair = []
            for p in range(2):
                value = field[s][c][p]
                if from_low:
                    hop = jnp.where(inner_low, turned(value, -shape.blocks, 0), 0.0)
                else:
                    hop = jnp.where(inner_high, turned(value, shape.blocks, 0), 0.0)
                pair.append((5.0 - wall_height) * value - 0.5 * total[s][c][p] - hop)
            colours.append(tuple(pair))
        result.append(colours)
    store_parts(part_ref, result)


def raw_slice(ref, j):
    return [[tuple(ref[j, (s * 3 + c) * 2 + p] for p in range(2)) for c in range(3)] for s in range(4)]


def neighbour_slice(shape, place, ref):
    return pick(place.fifth_even, raw_slice(ref, shape.slices - 1), raw_slice(ref, 0))


def own_edge(shape, place, ref):
    field = load_field(ref)
    first = cut(field, 0, shape.blocks)
    last = cut(field, shape.rows - shape.blocks, shape.rows)
    return pick(place.fifth_even, first, last)


def neighbour_kernel(shape, mirror_ref, origin_ref, wide_ref, part_ref):
    place = Place()
    near = neighbour_slice(shape, place, mirror_ref)
    beyond = pick(place.fifth_even, raw_slice(mirror_ref, shape.slices - 2), raw_slice(mirror_ref, 1))
    edge = own_edge(shape, place, origin_ref)
    mass = jnp.where(place.fifth_even, place.low_mass, place.high_mass)
    edge = [[tuple(v * mass for v in pair) for pair in spin] for spin in edge]
    below = pick(place.fifth_even, beyond, edge)
    above = pick(place.fifth_even, edge, beyond)
    field = [[tuple(jnp.concatenate([v] * shape.slices, axis=0) for v in pair) for pair in spin] for spin in near]
    total = cut(space_hops(shape, field, wide_ref), 0, shape.blocks)
    result = []
    for s in range(4):
        hop = below if s < 2 else above
        result.append(
            [
                tuple((5.0 - wall_height) * near[s][c][p] - 0.5 * total[s][c][p] - hop[s][c][p] for p in range(2))
                for c in range(3)
            ]
        )
    store_parts(part_ref, result)


def store_packed(shape, ref, parts):
    for s, colours in enumerate(parts):
        for c, pair in enumerate(colours):
            for p, value in enumerate(pair):
                place, row = divmod((s * 3 + c) * 2 + p, shape.slices)
                ref[12 + place, row * shape.blocks : (row + 1) * shape.blocks] = value


def load_packed(shape, ref):
    def part(index):
        place, row = divmod(index, shape.slices)
        return ref[12 + place, row * shape.blocks : (row + 1) * shape.blocks]

    return [[tuple(part((s * 3 + c) * 2 + p) for p in range(2)) for c in range(3)] for s in range(2)]


def send_neighbour(shape, place, mirror_ref, link, near_ref, far_ref):
    field = neighbour_slice(shape, place, mirror_ref)
    ahead = project(field, TIME, -1.0)
    behind = colour_mul(cut(link, 0, shape.blocks), project(field, TIME, 1.0), True)
    store_packed(shape, far_ref, pick(place.even, ahead, behind))
    store_packed(shape, near_ref, pick(place.even, behind, ahead))


def computed_across(shape, place, link, near_ref, far_ref, part_ref, origin_ref, scale, weight):
    near, far = load_packed(shape, near_ref), load_packed(shape, far_ref)
    ahead = colour_mul(cut(link, 0, shape.blocks), pick(place.even, near, far), False)
    behind = pick(place.even, far, near)
    ahead = [[tuple(v * place.high_sign for v in pair) for pair in spin] for spin in ahead]
    behind = [[tuple(v * place.low_sign for v in pair) for pair in spin] for spin in behind]
    zero = jnp.zeros((shape.blocks, LANES), jnp.float32)
    total = [[(zero, zero) for _ in range(3)] for _ in range(4)]
    add_rebuilt(total, ahead, TIME, -1.0)
    add_rebuilt(total, behind, TIME, 1.0)
    start, part = own_edge(shape, place, origin_ref), load_field(part_ref)
    result = []
    for s in range(4):
        sign = scale if s < 2 else -scale
        result.append(
            [
                tuple(weight * start[s][c][p] + sign * (part[s][c][p] - 0.5 * total[s][c][p]) for p in range(2))
                for c in range(3)
            ]
        )
    return pick(place.fifth_even, result[2:4], result[0:2])


def close_kernel(
    shape, odd_step, scale, weight, last, part_ref, wide_ref, start_ref, near_ref, far_ref, side_ref, across_ref,
    neighbour, out_refs
):
    place = Place()
    even = place.even
    link = load_link(wide_ref, TIME)
    near, far = load_half(near_ref), load_half(far_ref)
    ahead = colour_mul(link, pick(even, near, far), False)
    behind = pick(even, far, near)
    zero = jnp.zeros((shape.rows, LANES), jnp.float32)
    total = [[(zero, zero) for _ in range(3)] for _ in range(4)]
    ahead = [[tuple(v * place.high_sign for v in pair) for pair in spin] for spin in ahead]
    behind = [[tuple(v * place.low_sign for v in pair) for pair in spin] for spin in behind]
    add_rebuilt(total, ahead, TIME, -1.0)
    add_rebuilt(total, behind, TIME, 1.0)
    start = load_field(start_ref) if odd_step else raw_field(shape, start_ref, True)
    side = load_half(side_ref)
    if neighbour is not None:
        across = computed_across(shape, place, link, near_ref, far_ref, neighbour[0], start_ref, *neighbour[1:])
    elif across_ref is None:
        final = [[tuple(start_ref[shape.slices - 1, (s * 3 + c) * 2 + p] for p in range(2)) for c in range(3)] for s in range(2)]
        first = [[tuple(start_ref[0, (s * 3 + c) * 2 + p] for p in range(2)) for c in range(3)] for s in range(2, 4)]
        across = pick(place.fifth_even, final, first)
    else:
        across = load_half(across_ref)
    low = pick(place.fifth_even, across, side)
    high = pick(place.fifth_even, side, across)
    rest = jnp.zeros((shape.rows - shape.blocks, LANES), jnp.float32)
    field = []
    for s in range(4):
        from_low = (s < 2) != odd_step
        sign = scale if s < 2 else -scale
        colours = []
        for c in range(3):
            pair = []
            for p in range(2):
                index = (s * 3 + c) * 2 + p
                if from_low:
                    hop = jnp.concatenate([low[s % 2][c][p] * place.low_mass, rest], axis=0)
                else:
                    hop = jnp.concatenate([rest, high[s % 2][c][p] * place.high_mass], axis=0)
                value = part_ref[index] - 0.5 * total[s][c][p] - hop
                pair.append(weight * start[s][c][p] + sign * value)
            colours.append(tuple(pair))
        field.append(colours)
    if last:
        (out_ref,) = out_refs
        for s in range(4):
            for c in range(3):
                for p in range(2):
                    for j in range(shape.slices):
                        out_ref[j, (s * 3 + c) * 2 + p] = field[s][c][p][j * shape.blocks : (j + 1) * shape.blocks]
        return
    field_ref, near_out, far_out, side_out, *across_out = out_refs
    across_out = across_out[0] if across_out else None
    send_parts(shape, field, link, place, not odd_step, near_out, far_out, side_out, across_out)
    if across_out is None:
        send_neighbour(shape, place, start_ref, link, near_out, far_out)
    store_parts(field_ref, field)


def on_device(spinor, gauge_links):
    slices, _, depth, sites = spinor.shape
    space_count = lax.axis_size("space")
    fifth_count = lax.axis_size("fifth")
    assert depth == 1 and DEGREE % 2 == 0 and space_count % 2 == 0 and fifth_count % 2 == 0
    shape = Shape(slices, sites)
    rows, blocks = shape.rows, shape.blocks
    near_pairs = [(i, i ^ 1) for i in range(space_count)]
    far_pairs = [(i, (i + (1 if i % 2 else -1)) % space_count) for i in range(space_count)]
    side_pairs = [(i, i ^ 1) for i in range(fifth_count)]
    across_pairs = [(i, (i + (1 if i % 2 else -1)) % fifth_count) for i in range(fifth_count)]
    mirror_pairs = [(i, fifth_count - 1 - i) for i in range(fifth_count)]
    first_across = across_pairs != mirror_pairs or slices < 2

    vmem = pl.BlockSpec(memory_space=pltpu.VMEM)
    hbm = pl.BlockSpec(memory_space=pltpu.HBM)

    def array(*dims):
        return jax.ShapeDtypeStruct(dims, jnp.float32)

    def call(body, out_shape, *operands, operand_specs=None, scratch=()):
        return pl.pallas_call(
            body,
            out_shape=out_shape,
            in_specs=operand_specs or [vmem] * len(operands),
            out_specs=jax.tree.map(lambda _: vmem, out_shape),
            scratch_shapes=scratch,
            compiler_params=pltpu.CompilerParams(vmem_limit_bytes=VMEM_GRANT),
        )(*operands)

    whole, half, edge = array(24, rows, LANES), array(12, rows, LANES), array(12, blocks, LANES)
    weights = power_coefficients(DEGREE)
    start = spinor.reshape(slices, 24, blocks, LANES)
    links = gauge_links.reshape(4, 18, blocks, LANES)
    table = pl.pallas_call(
        table_kernel,
        out_shape=array(8, LANES),
        out_specs=vmem,
        cost_estimate=pl.CostEstimate(flops=TABLE_FLOPS, bytes_accessed=4096, transcendentals=0),
        compiler_params=pltpu.CompilerParams(vmem_limit_bytes=VMEM_GRANT),
    )()
    mirrored = lax.ppermute(start, "fifth", mirror_pairs)

    def first(spinor_ref, links_ref, table_ref, field_ref, near_ref, far_ref, side_ref, *rest):
        across_ref = rest[0] if first_across else None
        first_kernel(shape, spinor_ref, links_ref, table_ref, field_ref, near_ref, far_ref, side_ref, across_ref, *rest[-2:])

    sends = (whole, half, half, edge) + ((edge,) if first_across else ())
    scratch = (pltpu.VMEM((18, rows, LANES), jnp.float32), pltpu.SemaphoreType.DMA((2 * slices,)))
    origin, near, far, side, *across = call(first, sends, start, links, table, operand_specs=(hbm, hbm, vmem), scratch=scratch)
    field, wide = origin, None
    for step in range(DEGREE):
        odd_step, last = step % 2 == 1, step == DEGREE - 1
        far_in = lax.ppermute(far, "space", far_pairs)
        across_in = [lax.ppermute(value, "fifth", across_pairs) for value in across]
        side_in = lax.ppermute(side, "fifth", side_pairs)
        near_in = lax.ppermute(near, "space", near_pairs)
        if wide is None:
            wide = call(lambda *refs: widen_kernel(shape, *refs), array(72, rows, LANES), links)
        part = call(lambda *refs, odd=odd_step: space_kernel(shape, odd, *refs), whole, field, wide)
        scale = weights[DEGREE] if step == 0 else 1.0
        computed = step == 1 and not first_across
        if computed:
            extra = (call(lambda *refs: neighbour_kernel(shape, *refs), array(24, blocks, LANES), mirrored, origin, wide),)
        else:
            extra = tuple(across_in)

        def close(*refs, step=step, odd=odd_step, last=last, scale=scale, computed=computed, count=len(extra)):
            across_ref = refs[6] if count and not computed else None
            neighbour = (refs[6], weights[DEGREE], weights[DEGREE - 1]) if computed else None
            weight = weights[DEGREE - 1 - step]
            close_kernel(shape, odd, scale, weight, last, *refs[:6], across_ref, neighbour, refs[6 + count :])

        operands = (part, wide, origin if odd_step else mirrored, near_in, far_in, side_in, *extra)
        if last:
            result = call(close, array(slices, 24, blocks, LANES), *operands)
        elif step == 0 and not first_across:
            more = array(12 + -(-12 // slices), rows, LANES)
            field, near, far, side, *across = call(close, (whole, more, more, edge), *operands)
        else:
            field, near, far, side, *across = call(close, (whole, half, half, edge, edge), *operands)
    return result.reshape(slices, 24, depth, sites)


def solution(mesh):
    placed = (P("fifth", None, "space", None), P(None, None, "space", None))
    return jax.shard_map(
        on_device,
        mesh=mesh,
        in_specs=placed,
        out_specs=P("fifth", None, "space", None),
        check_vma=False,
    )
```

```python
import jax
import jax.numpy as jnp
import numpy as np
from jax import lax
from jax.experimental import pallas as pl
from jax.experimental.pallas import tpu as pltpu
from jax.sharding import PartitionSpec as P

DEGREE = 4
LANES = 128
VMEM_GRANT = 8 * 2**20
TABLE_FLOPS = 10**8

wall_height = 1.8
quark_mass = 0.1
filter_center = 0.5
filter_radius = 8.0
gamma_block = (((1, 1), (0, 1)), ((1, 2), (0, 0)), ((0, 1), (1, 3)), ((0, 0), (1, 0)))
gamma_adjoint = (((1, 3), (0, 3)), ((1, 0), (0, 2)), ((0, 3), (1, 1)), ((0, 0), (1, 0)))
TIME = 3


def power_coefficients(degree):
    series = np.polynomial.chebyshev.cheb2poly([0.0] * degree + [1.0])
    line = np.polynomial.Polynomial([-filter_center / filter_radius, 1.0 / filter_radius])
    total = np.polynomial.Polynomial([0.0])
    for order, weight in enumerate(series):
        total = total + weight * line**order
    return [float(value) for value in total.coef]


def plus_unit(base, other, quarter, parity):
    turn = (quarter + (2 if parity < 0 else 0)) % 4
    if turn == 0:
        return base[0] + other[0], base[1] + other[1]
    if turn == 1:
        return base[0] - other[1], base[1] + other[0]
    if turn == 2:
        return base[0] - other[0], base[1] - other[1]
    return base[0] + other[1], base[1] - other[0]


def project(field, direction, parity):
    halves = []
    for row in range(2):
        source, quarter = gamma_block[direction][row]
        halves.append(
            [plus_unit(field[row][c], field[2 + source][c], quarter, parity) for c in range(3)]
        )
    return halves


def add_rebuilt(total, half, direction, parity):
    for row in range(2):
        source, quarter = gamma_adjoint[direction][row]
        for c in range(3):
            total[row][c] = (total[row][c][0] + half[row][c][0], total[row][c][1] + half[row][c][1])
            total[2 + row][c] = plus_unit(total[2 + row][c], half[source][c], quarter, parity)


def colour_mul(link, half, dagger):
    result = []
    for spin in range(2):
        rows = []
        for row in range(3):
            total = None
            for column in range(3):
                h_re, h_im = half[spin][column]
                if dagger:
                    l_re, l_im = link[column][row]
                    t_re = l_re * h_re + l_im * h_im
                    t_im = l_re * h_im - l_im * h_re
                else:
                    l_re, l_im = link[row][column]
                    t_re = l_re * h_re - l_im * h_im
                    t_im = l_re * h_im + l_im * h_re
                total = (t_re, t_im) if total is None else (total[0] + t_re, total[1] + t_im)
            rows.append(total)
        result.append(rows)
    return result


class Shape:
    def __init__(self, slices, sites):
        self.slices = slices
        self.sites = sites
        self.blocks = sites // LANES
        self.rows = slices * self.blocks
        self.extent = round(sites ** (1.0 / 3.0))
        assert self.extent**3 == sites and sites % LANES == 0


def index_of(shape, axis):
    return lax.broadcasted_iota(jnp.int32, (shape.rows, LANES), axis)


def turned(value, steps, axis):
    size = value.shape[axis]
    if steps % size == 0:
        return value
    return pltpu.roll(value, (-steps) % size, axis)


def space_shift(shape, stride, forward):
    extent = shape.extent
    group = stride * extent
    sign = 1 if forward else -1
    lane = index_of(shape, 1)
    if LANES % group == 0:
        place = lane // stride % extent
        edge = place == (extent - 1 if forward else 0)
        return lambda v: jnp.where(
            edge, turned(v, -sign * (extent - 1) * stride, 1), turned(v, sign * stride, 1)
        )
    assert group == shape.sites and stride < LANES
    block = index_of(shape, 0) % shape.blocks
    wraps = block == (shape.blocks - 1 if forward else 0)
    stays = lane < LANES - stride if forward else lane >= stride

    def shift(v):
        across = turned(v, sign * stride, 1)
        other = jnp.where(
            wraps, turned(across, -sign * (shape.blocks - 1), 0), turned(across, sign, 0)
        )
        return jnp.where(stays, across, other)

    return shift


def load_field(ref):
    return [[(ref[(s * 3 + c) * 2], ref[(s * 3 + c) * 2 + 1]) for c in range(3)] for s in range(4)]


def load_half(ref):
    return [[(ref[(s * 3 + c) * 2], ref[(s * 3 + c) * 2 + 1]) for c in range(3)] for s in range(2)]


def store_parts(ref, parts, rows=None):
    for s, colours in enumerate(parts):
        for c, pair in enumerate(colours):
            for p, value in enumerate(pair):
                if rows is None:
                    ref[(s * 3 + c) * 2 + p] = value
                else:
                    ref[(s * 3 + c) * 2 + p] = value[rows[0] : rows[1]]


def load_link(ref, direction):
    return [
        [(ref[direction * 18 + (r * 3 + c) * 2], ref[direction * 18 + (r * 3 + c) * 2 + 1]) for c in range(3)]
        for r in range(3)
    ]


def raw_field(shape, ref, mirrored):
    order = range(shape.slices)
    if mirrored:
        order = reversed(order)
    order = list(order)

    def part(index):
        return jnp.concatenate([ref[j, index] for j in order], axis=0)

    return [[(part((s * 3 + c) * 2), part((s * 3 + c) * 2 + 1)) for c in range(3)] for s in range(4)]


def cut(parts, low, high):
    return [[tuple(v[low:high] for v in pair) for pair in spin] for spin in parts]


def pick(flag, first, second):
    return [
        [tuple(jnp.where(flag, a, b) for a, b in zip(p, q)) for p, q in zip(x, y)]
        for x, y in zip(first, second)
    ]


class Place:
    def __init__(self):
        space, fifth = lax.axis_index("space"), lax.axis_index("fifth")
        last_space, last_fifth = lax.axis_size("space") - 1, lax.axis_size("fifth") - 1
        self.even = space % 2 == 0
        self.fifth_even = fifth % 2 == 0
        self.low_sign = jnp.where(space == 0, -1.0, 1.0)
        self.high_sign = jnp.where(space == last_space, -1.0, 1.0)
        self.low_mass = jnp.where(fifth == 0, -quark_mass, 1.0)
        self.high_mass = jnp.where(fifth == last_fifth, -quark_mass, 1.0)


def send_parts(shape, field, link, place, odd_step, near_ref, far_ref, side_ref, across_ref):
    ahead = project(field, TIME, -1.0)
    behind = colour_mul(link, project(field, TIME, 1.0), True)
    store_parts(far_ref, pick(place.even, ahead, behind))
    upper, lower = field[0:2], field[2:4]
    up = cut(lower if odd_step else upper, shape.rows - shape.blocks, shape.rows)
    down = cut(upper if odd_step else lower, 0, shape.blocks)
    if across_ref is not None:
        store_parts(across_ref, pick(place.fifth_even, down, up))
    store_parts(side_ref, pick(place.fifth_even, up, down))
    store_parts(near_ref, pick(place.even, behind, ahead))


def widen_kernel(shape, links_ref, wide_ref):
    for mu in range(4):
        for index in range(18):
            value = links_ref[mu, index]
            wide_ref[mu * 18 + index] = jnp.concatenate([value] * shape.slices, axis=0)


def table_kernel(table_ref):
    place = Place()
    even = jnp.where(place.even, 1.0, 0.0)
    values = (even, place.low_sign, place.high_sign, place.low_mass, place.high_mass)
    for row, value in enumerate(values):
        table_ref[row : row + 1] = jnp.full((1, LANES), value, jnp.float32)
    table_ref[len(values) :] = jnp.zeros((8 - len(values), LANES), jnp.float32)


def first_kernel(shape, spinor_ref, links_ref, table_ref, field_ref, near_ref, far_ref, side_ref, across_ref, link_ref, sems):
    copies = []
    for j in range(shape.slices):
        part = pl.ds(j * shape.blocks, shape.blocks)
        copies.append((spinor_ref.at[j], field_ref.at[:, part]))
        copies.append((links_ref.at[TIME], link_ref.at[:, part]))
    copies = [pltpu.make_async_copy(a, b, sems.at[i]) for i, (a, b) in enumerate(copies)]
    for copy in copies:
        copy.start()
    for copy in copies:
        copy.wait()
    place = Place()
    place.even = table_ref[0:1] > 0.5
    field, link = load_field(field_ref), load_link(link_ref, 0)
    send_parts(shape, field, link, place, False, near_ref, far_ref, side_ref, across_ref)


def space_hops(shape, field, wide_ref):
    zero = jnp.zeros((shape.rows, LANES), jnp.float32)
    total = [[(zero, zero) for _ in range(3)] for _ in range(4)]
    for mu in range(3):
        stride = shape.extent**mu
        link = load_link(wide_ref, mu)
        ahead = space_shift(shape, stride, True)
        half = project(field, mu, -1.0)
        half = [[tuple(ahead(v) for v in pair) for pair in spin] for spin in half]
        add_rebuilt(total, colour_mul(link, half, False), mu, -1.0)
        behind = space_shift(shape, stride, False)
        half = colour_mul(link, project(field, mu, 1.0), True)
        half = [[tuple(behind(v) for v in pair) for pair in spin] for spin in half]
        add_rebuilt(total, half, mu, 1.0)
    return total


def space_kernel(shape, odd_step, field_ref, wide_ref, part_ref):
    field = load_field(field_ref)
    total = space_hops(shape, field, wide_ref)
    row = index_of(shape, 0)
    inner_low = row >= shape.blocks
    inner_high = row < shape.rows - shape.blocks
    result = []
    for s in range(4):
        from_low = (s < 2) != odd_step
        colours = []
        for c in range(3):
            pair = []
            for p in range(2):
                value = field[s][c][p]
                if from_low:
                    hop = jnp.where(inner_low, turned(value, -shape.blocks, 0), 0.0)
                else:
                    hop = jnp.where(inner_high, turned(value, shape.blocks, 0), 0.0)
                pair.append((5.0 - wall_height) * value - 0.5 * total[s][c][p] - hop)
            colours.append(tuple(pair))
        result.append(colours)
    store_parts(part_ref, result)


def slice_of(shape, ref, j):
    def part(index):
        if len(ref.shape) == 4:
            return ref[j, index]
        return ref[index, j * shape.blocks : (j + 1) * shape.blocks]

    return [[tuple(part((s * 3 + c) * 2 + p) for p in range(2)) for c in range(3)] for s in range(4)]


def neighbour_slice(shape, place, ref):
    return pick(place.fifth_even, slice_of(shape, ref, shape.slices - 1), slice_of(shape, ref, 0))


def own_edge(shape, place, ref):
    field = load_field(ref)
    first = cut(field, 0, shape.blocks)
    last = cut(field, shape.rows - shape.blocks, shape.rows)
    return pick(place.fifth_even, first, last)


def neighbour_kernel(shape, across_ref, field_ref, wide_ref, part_ref):
    place = Place()
    near = neighbour_slice(shape, place, across_ref)
    beyond = pick(place.fifth_even, slice_of(shape, across_ref, shape.slices - 2), slice_of(shape, across_ref, 1))
    edge = own_edge(shape, place, field_ref)
    mass = jnp.where(place.fifth_even, place.low_mass, place.high_mass)
    edge = [[tuple(v * mass for v in pair) for pair in spin] for spin in edge]
    below = pick(place.fifth_even, beyond, edge)
    above = pick(place.fifth_even, edge, beyond)
    field = [[tuple(jnp.concatenate([v] * shape.slices, axis=0) for v in pair) for pair in spin] for spin in near]
    total = cut(space_hops(shape, field, wide_ref), 0, shape.blocks)
    result = []
    for s in range(4):
        hop = below if s < 2 else above
        result.append(
            [
                tuple((5.0 - wall_height) * near[s][c][p] - 0.5 * total[s][c][p] - hop[s][c][p] for p in range(2))
                for c in range(3)
            ]
        )
    store_parts(part_ref, result)


def store_packed(shape, ref, parts):
    for s, colours in enumerate(parts):
        for c, pair in enumerate(colours):
            for p, value in enumerate(pair):
                place, row = divmod((s * 3 + c) * 2 + p, shape.slices)
                ref[12 + place, row * shape.blocks : (row + 1) * shape.blocks] = value


def load_packed(shape, ref):
    def part(index):
        place, row = divmod(index, shape.slices)
        return ref[12 + place, row * shape.blocks : (row + 1) * shape.blocks]

    return [[tuple(part((s * 3 + c) * 2 + p) for p in range(2)) for c in range(3)] for s in range(2)]


def send_neighbour(shape, place, across_ref, link, near_ref, far_ref):
    field = neighbour_slice(shape, place, across_ref)
    ahead = project(field, TIME, -1.0)
    behind = colour_mul(cut(link, 0, shape.blocks), project(field, TIME, 1.0), True)
    store_packed(shape, far_ref, pick(place.even, ahead, behind))
    store_packed(shape, near_ref, pick(place.even, behind, ahead))


def computed_across(shape, place, link, near_ref, far_ref, part_ref, origin_ref, scale, weight):
    near, far = load_packed(shape, near_ref), load_packed(shape, far_ref)
    ahead = colour_mul(cut(link, 0, shape.blocks), pick(place.even, near, far), False)
    behind = pick(place.even, far, near)
    ahead = [[tuple(v * place.high_sign for v in pair) for pair in spin] for spin in ahead]
    behind = [[tuple(v * place.low_sign for v in pair) for pair in spin] for spin in behind]
    zero = jnp.zeros((shape.blocks, LANES), jnp.float32)
    total = [[(zero, zero) for _ in range(3)] for _ in range(4)]
    add_rebuilt(total, ahead, TIME, -1.0)
    add_rebuilt(total, behind, TIME, 1.0)
    start, part = own_edge(shape, place, origin_ref), load_field(part_ref)
    result = []
    for s in range(4):
        sign = scale if s < 2 else -scale
        result.append(
            [
                tuple(weight * start[s][c][p] + sign * (part[s][c][p] - 0.5 * total[s][c][p]) for p in range(2))
                for c in range(3)
            ]
        )
    return pick(place.fifth_even, result[2:4], result[0:2])


def close_kernel(
    shape, odd_step, scale, weight, last, part_ref, wide_ref, start_ref, near_ref, far_ref, side_ref, across_ref,
    neighbour, out_refs
):
    place = Place()
    even = place.even
    link = load_link(wide_ref, TIME)
    near, far = load_half(near_ref), load_half(far_ref)
    ahead = colour_mul(link, pick(even, near, far), False)
    behind = pick(even, far, near)
    zero = jnp.zeros((shape.rows, LANES), jnp.float32)
    total = [[(zero, zero) for _ in range(3)] for _ in range(4)]
    ahead = [[tuple(v * place.high_sign for v in pair) for pair in spin] for spin in ahead]
    behind = [[tuple(v * place.low_sign for v in pair) for pair in spin] for spin in behind]
    add_rebuilt(total, ahead, TIME, -1.0)
    add_rebuilt(total, behind, TIME, 1.0)
    start = load_field(start_ref) if odd_step else raw_field(shape, start_ref, True)
    side = load_half(side_ref)
    if neighbour is not None:
        across = computed_across(shape, place, link, near_ref, far_ref, neighbour[0], start_ref, *neighbour[1:])
    elif 24 in across_ref.shape[:2]:
        final, first = slice_of(shape, across_ref, shape.slices - 1), slice_of(shape, across_ref, 0)
        across = pick(place.fifth_even, final[0:2], first[2:4])
    else:
        across = load_half(across_ref)
    low = pick(place.fifth_even, across, side)
    high = pick(place.fifth_even, side, across)
    rest = jnp.zeros((shape.rows - shape.blocks, LANES), jnp.float32)
    field = []
    for s in range(4):
        from_low = (s < 2) != odd_step
        sign = scale if s < 2 else -scale
        colours = []
        for c in range(3):
            pair = []
            for p in range(2):
                index = (s * 3 + c) * 2 + p
                if from_low:
                    hop = jnp.concatenate([low[s % 2][c][p] * place.low_mass, rest], axis=0)
                else:
                    hop = jnp.concatenate([rest, high[s % 2][c][p] * place.high_mass], axis=0)
                value = part_ref[index] - 0.5 * total[s][c][p] - hop
                pair.append(weight * start[s][c][p] + sign * value)
            colours.append(tuple(pair))
        field.append(colours)
    if last:
        (out_ref,) = out_refs
        for s in range(4):
            for c in range(3):
                for p in range(2):
                    for j in range(shape.slices):
                        out_ref[j, (s * 3 + c) * 2 + p] = field[s][c][p][j * shape.blocks : (j + 1) * shape.blocks]
        return
    field_ref, near_out, far_out, side_out, *across_out = out_refs
    across_out = across_out[0] if across_out else None
    send_parts(shape, field, link, place, not odd_step, near_out, far_out, side_out, across_out)
    if across_out is None and not odd_step:
        send_neighbour(shape, place, across_ref, link, near_out, far_out)
    store_parts(field_ref, field)


def on_device(spinor, gauge_links):
    slices, _, depth, sites = spinor.shape
    space_count = lax.axis_size("space")
    fifth_count = lax.axis_size("fifth")
    assert depth == 1 and DEGREE % 2 == 0 and space_count % 2 == 0 and fifth_count % 2 == 0
    shape = Shape(slices, sites)
    rows, blocks = shape.rows, shape.blocks
    near_pairs = [(i, i ^ 1) for i in range(space_count)]
    far_pairs = [(i, (i + (1 if i % 2 else -1)) % space_count) for i in range(space_count)]
    side_pairs = [(i, i ^ 1) for i in range(fifth_count)]
    across_pairs = [(i, (i + (1 if i % 2 else -1)) % fifth_count) for i in range(fifth_count)]
    mirror_pairs = [(i, fifth_count - 1 - i) for i in range(fifth_count)]
    first_across = across_pairs != mirror_pairs or slices < 2

    vmem = pl.BlockSpec(memory_space=pltpu.VMEM)
    hbm = pl.BlockSpec(memory_space=pltpu.HBM)

    def array(*dims):
        return jax.ShapeDtypeStruct(dims, jnp.float32)

    def call(body, out_shape, *operands, operand_specs=None, scratch=()):
        return pl.pallas_call(
            body,
            out_shape=out_shape,
            in_specs=operand_specs or [vmem] * len(operands),
            out_specs=jax.tree.map(lambda _: vmem, out_shape),
            scratch_shapes=scratch,
            compiler_params=pltpu.CompilerParams(vmem_limit_bytes=VMEM_GRANT),
        )(*operands)

    whole, half, edge = array(24, rows, LANES), array(12, rows, LANES), array(12, blocks, LANES)
    weights = power_coefficients(DEGREE)
    start = spinor.reshape(slices, 24, blocks, LANES)
    links = gauge_links.reshape(4, 18, blocks, LANES)
    table = pl.pallas_call(
        table_kernel,
        out_shape=array(8, LANES),
        out_specs=vmem,
        cost_estimate=pl.CostEstimate(flops=TABLE_FLOPS, bytes_accessed=4096, transcendentals=0),
        compiler_params=pltpu.CompilerParams(vmem_limit_bytes=VMEM_GRANT),
    )()
    mirrored = lax.ppermute(start, "fifth", mirror_pairs)

    def first(spinor_ref, links_ref, table_ref, field_ref, near_ref, far_ref, side_ref, *rest):
        across_ref = rest[0] if first_across else None
        first_kernel(shape, spinor_ref, links_ref, table_ref, field_ref, near_ref, far_ref, side_ref, across_ref, *rest[-2:])

    sends = (whole, half, half, edge) + ((edge,) if first_across else ())
    scratch = (pltpu.VMEM((18, rows, LANES), jnp.float32), pltpu.SemaphoreType.DMA((2 * slices,)))
    origin, near, far, side, *across = call(first, sends, start, links, table, operand_specs=(hbm, hbm, vmem), scratch=scratch)
    field, wide, across_whole = origin, None, mirrored
    for step in range(DEGREE):
        odd_step, last = step % 2 == 1, step == DEGREE - 1
        if not first_across:
            across = [field] if step > 0 and not odd_step else []
        far_in = lax.ppermute(far, "space", far_pairs)
        across_in = [lax.ppermute(value, "fifth", across_pairs) for value in across]
        side_in = lax.ppermute(side, "fifth", side_pairs)
        near_in = lax.ppermute(near, "space", near_pairs)
        if wide is None:
            wide = call(lambda *refs: widen_kernel(shape, *refs), array(72, rows, LANES), links)
        part = call(lambda *refs, odd=odd_step: space_kernel(shape, odd, *refs), whole, field, wide)
        scale = weights[DEGREE] if step == 0 else 1.0
        computed = odd_step and not first_across
        if computed:
            extra = call(
                lambda *refs: neighbour_kernel(shape, *refs), array(24, blocks, LANES), across_whole, across_field, wide
            )
        elif first_across:
            (extra,) = across_in
        else:
            across_whole = across_in[0] if step > 0 else mirrored
            extra, across_field = across_whole, field

        def close(*refs, step=step, odd=odd_step, last=last, scale=scale, computed=computed):
            across_ref = None if computed else refs[6]
            neighbour = (refs[6], weights[DEGREE] if step == 1 else 1.0, weights[DEGREE - step]) if computed else None
            weight = weights[DEGREE - 1 - step]
            close_kernel(shape, odd, scale, weight, last, *refs[:6], across_ref, neighbour, refs[7:])

        operands = (part, wide, origin if odd_step else mirrored, near_in, far_in, side_in, extra)
        if last:
            result = call(close, array(slices, 24, blocks, LANES), *operands)
        elif first_across:
            field, near, far, side, *across = call(close, (whole, half, half, edge, edge), *operands)
        else:
            message = half if odd_step else array(12 + -(-12 // slices), rows, LANES)
            field, near, far, side = call(close, (whole, message, message, edge), *operands)
    return result.reshape(slices, 24, depth, sites)


def solution(mesh):
    placed = (P("fifth", None, "space", None), P(None, None, "space", None))
    return jax.shard_map(
        on_device,
        mesh=mesh,
        in_specs=placed,
        out_specs=P("fifth", None, "space", None),
        check_vma=False,
    )
```
